32 devices in a mesh: groups: 2 (over x), head: 8 (over z, y), tensor: 2 (over core).
Axes of the slice: x: 2, y: 2, z: 4, core: 2. Of those that a mesh axis runs over, the one named last changes fastest.
Arguments:
- query: bfloat16 [8192, 1024], P(('groups', 'head'), 'tensor'), parts along dimension 0, may hold values from -32 to 32
- keys_in: bfloat16 [8192, 1024], P(('groups', 'head'), 'tensor'), parts along dimension 0, may hold values from -6 to 6
- values_in: bfloat16 [8192, 1024], P(('groups', 'head'), 'tensor'), parts along dimension 0, may hold values from -6 to 6
- grad_out: bfloat16 [8192, 1024], P(('groups', 'head'), 'tensor'), parts along dimension 0, may hold values from -96 to 96
- w_out: bfloat16 [1024, 1024], P('tensor'), may hold values from -0.1875 to 0.1875
- w_query: bfloat16 [1024, 1024], P(None, 'tensor'), may hold values from -0.1875 to 0.1875
- w_key: bfloat16 [1024, 1024], P(None, 'tensor'), may hold values from -0.1875 to 0.1875
- w_value: bfloat16 [1024, 1024], P(None, 'tensor'), may hold values from -0.1875 to 0.1875
- perm: int32 [2, 4096], P('groups'), parts along dimension 0, may hold values from 0 to 4095, as said below
- blocks: int32 [2, 32, 12], P('groups'), parts along dimension 0, may hold values from 0 to 31, as said below
- counts: int32 [2, 32], P('groups'), parts along dimension 0, may hold values from 1 to 12
Outputs:
- input_grad: bfloat16 [8192, 1024], P(('groups', 'head', 'tensor')), parts along dimension 0
The draws below stay inside these ranges and needn't reach their ends.
There are 2 independent parts, one for each index of `groups`. The reference program is written for one: setup_inputs(seed, part) draws one part's arguments, and reference() takes and returns one part's arrays. A program takes and returns all parts, laid end to end along the dimension named above; an argument that names none is the same for every part. Nothing has to cross between parts.
Inputs may be any that keep to these rules, and one draw needn't show every extreme that they name: Each row of perm holds every node number of the graph once. blocks[g, b, 0] is b; the 12 entries of blocks[g, b] are different block numbers.
All inputs are finite; a program needn't handle non-finite values.
Results may differ from the reference program's by a relative error of at most 0.011.
Values may be sent and summed in bfloat16 or wider, within the bound.
A program may use at most 64 MiB of HBM per device.

```python
import jax
import jax.numpy as jnp
from jax import lax

H = 16
HD = 64
D = 1024
BS = 128
KB = 12
PARTITIONS = 8
G = 1
R = 512
NG = 4096
NB = 32
NODES = 4096


def order_of(key):
    scores = jax.random.randint(jax.random.fold_in(key, 31), (G, NG), 0, 2 ** 16) * NG
    scores = scores + jnp.arange(NG, dtype=jnp.int32)[None, :]
    return jnp.argsort(scores, axis=1, stable=True).astype(jnp.int32)


def node_rows(values, order):
    width = values.shape[-1]
    placed = jnp.take_along_axis(values, order[:, :, None], axis=1)
    return placed.reshape(G, PARTITIONS, R, width).transpose(1, 2, 0, 3).reshape(NODES, width)


def draw_perm(key, part):
    return order_of(key)


def draw_keys_in(key, part):
    values = jnp.clip(jax.random.normal(jax.random.fold_in(key, 41), (G, NG, D), jnp.float32), -6.0, 6.0)
    return node_rows(values, order_of(key)).astype(jnp.bfloat16)


def draw_query(key, part):
    values = jnp.clip(jax.random.normal(jax.random.fold_in(key, 43), (G, NG, D), jnp.float32), -6.0, 6.0)
    return node_rows(values, order_of(key)).astype(jnp.bfloat16)


def draw_blocks(key, part):
    scores = jax.random.randint(jax.random.fold_in(key, 61), (G, NB, NB - 1), 0, 2 ** 16) * (NB - 1)
    scores = scores + jnp.arange(NB - 1, dtype=jnp.int32)[None, None, :]
    shifts = jnp.argsort(scores, axis=2, stable=True)[:, :, :KB - 1].astype(jnp.int32) + 1
    offsets = jnp.concatenate((jnp.zeros((G, NB, 1), jnp.int32), shifts), axis=2)
    return ((jnp.arange(NB, dtype=jnp.int32)[None, :, None] + offsets) % NB).astype(jnp.int32)


def draw_counts(key, part):
    drawn = jax.random.randint(jax.random.fold_in(key, 67), (G, NB), 1, KB + 1).astype(jnp.int32)
    drawn = drawn.at[:, 0].set(KB)
    return drawn.at[:, 1].set(1)


def level_of(rng, shape, split, smallest, largest):
    def one(axis_at, blocks):
        steps = jax.random.uniform(jax.random.fold_in(jax.random.fold_in(rng, 6), axis_at), (blocks,), jnp.float32, smallest / len(split), largest / len(split))
        return jnp.repeat(jnp.exp(steps), shape[axis_at] // blocks).reshape((-1,) + (1,) * (len(shape) - axis_at - 1))

    loudness = one(*split[0])
    for cut in split[1:]:
        loudness = loudness * one(*cut)
    return loudness


def centred(stream_key, shape, scale, limit, pieces=(), held_as=jnp.bfloat16):
    loudness = level_of(stream_key, shape, pieces, -0.22, 0.18) if pieces else 1.0
    values = jax.random.normal(stream_key, shape, jnp.float32) * scale * loudness
    return jnp.minimum(jnp.maximum(values, -limit), limit).astype(held_as)


def setup_inputs(seed: int = 0, part: int = 0) -> dict:
    key_list = jax.random.split(jax.random.key(seed), 12)
    own_keys = jax.random.split(jax.random.fold_in(key_list[11], part), 12)
    query = draw_query(jax.random.fold_in(jax.random.fold_in(key_list[11], part), 71), part)
    keys_in = draw_keys_in(jax.random.fold_in(jax.random.fold_in(key_list[11], part), 71), part)
    values_in = centred(own_keys[2], (NODES, D), 1.0, 6.0, ((0, 8), (1, 2)))
    grad_out = centred(own_keys[3], (NODES, D), 16.0, 96.0, ((0, 8), (1, 2)))
    w_out = centred(key_list[4], (D, D), D ** -0.5, 0.1875, ((0, 2),))
    w_query = centred(key_list[5], (D, D), D ** -0.5, 0.1875, ((1, 2),))
    w_key = centred(key_list[6], (D, D), D ** -0.5, 0.1875, ((1, 2),))
    w_value = centred(key_list[7], (D, D), D ** -0.5, 0.1875, ((1, 2),))
    perm = draw_perm(jax.random.fold_in(jax.random.fold_in(key_list[11], part), 71), part)
    blocks = draw_blocks(jax.random.fold_in(jax.random.fold_in(key_list[11], part), 71), part)
    counts = draw_counts(jax.random.fold_in(jax.random.fold_in(key_list[11], part), 71), part)
    return dict(query=query, keys_in=keys_in, values_in=values_in, grad_out=grad_out, w_out=w_out, w_query=w_query, w_key=w_key, w_value=w_value, perm=perm, blocks=blocks, counts=counts)


def to_graphs(values):
    width = values.shape[-1]
    return values.reshape(PARTITIONS, R, G, width).transpose(2, 0, 1, 3).reshape(G, NG, width)


def to_rows(values):
    width = values.shape[-1]
    return values.reshape(G, PARTITIONS, R, width).transpose(1, 2, 0, 3).reshape(NODES, width)


def head_grads(query_head, keys_head, values_head, grads_head, listed, active):
    scale = HD ** -0.5
    query_blk = query_head.reshape(NB, BS, HD).astype(jnp.float32)
    grad_blk = grads_head.reshape(NB, BS, HD).astype(jnp.float32)
    key_blk = keys_head.reshape(NB, BS, HD).astype(jnp.float32)
    value_blk = values_head.reshape(NB, BS, HD).astype(jnp.float32)
    fetched_keys = key_blk[listed]
    fetched_values = value_blk[listed]
    score = jnp.einsum("qad,qjcd->qajc", query_blk, fetched_keys) * scale
    score = jnp.where(active[:, None, :, None], score, -jnp.inf)
    top = jnp.max(score, axis=(2, 3), keepdims=True)
    expo = jnp.exp(score - top)
    prob = expo / jnp.sum(expo, axis=(2, 3), keepdims=True)
    prob_b = lax.optimization_barrier(prob.astype(jnp.bfloat16)).astype(jnp.float32)
    attn = jnp.einsum("qajc,qjcd->qad", prob_b, fetched_values)
    delta = jnp.sum(grad_blk * attn, axis=-1)
    dprob = jnp.einsum("qad,qjcd->qajc", grad_blk, fetched_values)
    dscore = prob * (dprob - delta[:, :, None, None])
    dscore = lax.optimization_barrier(dscore.astype(jnp.bfloat16)).astype(jnp.float32)
    query_grad = jnp.einsum("qajc,qjcd->qad", dscore, fetched_keys) * scale
    key_terms = jnp.einsum("qajc,qad->qjcd", dscore, query_blk) * scale
    value_terms = jnp.einsum("qajc,qad->qjcd", prob_b, grad_blk)
    key_grad = jnp.zeros((NB, BS, HD), jnp.float32).at[listed].add(key_terms)
    value_grad = jnp.zeros((NB, BS, HD), jnp.float32).at[listed].add(value_terms)
    joined = jnp.concatenate((query_grad.reshape(NG, HD), key_grad.reshape(NG, HD), value_grad.reshape(NG, HD)), axis=1)
    return joined.astype(jnp.bfloat16)


def reference(query, keys_in, values_in, grad_out, w_out, w_query, w_key, w_value, perm, blocks, counts):
    attn_grad = jnp.dot(grad_out, w_out.T, preferred_element_type=jnp.float32).astype(jnp.bfloat16)
    stacked = jnp.stack([to_graphs(item) for item in (query, keys_in, values_in, attn_grad)], axis=1)

    def per_graph(inputs):
        member, order, listed, count_row = inputs
        inverse = jnp.zeros((NG,), jnp.int32).at[order].set(jnp.arange(NG, dtype=jnp.int32))
        by_node = jnp.take(member, inverse, axis=1)
        by_head = by_node.reshape(4, NG, H, HD).transpose(2, 0, 1, 3)
        active = jnp.arange(KB, dtype=jnp.int32)[None, :] < count_row[:, None]

        def per_head(parts):
            return head_grads(parts[0], parts[1], parts[2], parts[3], listed, active)

        grads = lax.map(per_head, by_head)
        grads = grads.reshape(H, NG, 3, HD).transpose(1, 2, 0, 3).reshape(NG, 3 * D)
        return jnp.take(grads, order, axis=0)

    per_part = lax.map(per_graph, (stacked, perm, blocks, counts))
    all_rows = to_rows(per_part)
    total = jnp.dot(all_rows[:, :D], w_query.T, preferred_element_type=jnp.float32)
    total = total + jnp.dot(all_rows[:, D:2 * D], w_key.T, preferred_element_type=jnp.float32)
    total = total + jnp.dot(all_rows[:, 2 * D:], w_value.T, preferred_element_type=jnp.float32)
    return total.astype(jnp.bfloat16)
```

```python
import functools

import jax
import jax.numpy as jnp
from jax import lax
from jax.experimental import pallas as pl
from jax.experimental.pallas import tpu as pltpu
from jax.sharding import PartitionSpec as P

HD = 64
BS = 128
KB = 12
NT = (((1,), (1,)), ((), ()))
STEP = 4


def dot(a, b):
    return jnp.dot(a, b, preferred_element_type=jnp.float32)


def attend(block_ref, count_ref, row_ref, col_ref, x_ref, out_ref, kv_s, kt_s, qg_s, dkv_s, g_s, s_s, d_s):
    nodes = x_ref.shape[0]
    block_count = nodes // BS
    parts, out_rows, _ = out_ref.shape
    half = out_rows // 3
    scale = HD ** (-0.5)
    low = lax.broadcasted_iota(jnp.int32, (BS, 2 * HD), 1) < HD

    @pl.loop(0, block_count // 2)
    def _(i):
        ids = lax.broadcasted_iota(jnp.int32, (2 * BS, nodes), 0) + i * (2 * BS)
        hot = jnp.where(ids == row_ref[...], 1.0, 0.0).astype(jnp.bfloat16)
        got = dot(hot, x_ref[...])
        for u in range(2):
            b = i * 2 + u
            qg = got[u * BS:(u + 1) * BS, :2 * HD]
            kv = got[u * BS:(u + 1) * BS, 2 * HD:]
            qg_s[b, :BS] = jnp.where(low, qg * scale, 0.0).astype(jnp.bfloat16)
            qg_s[b, BS:] = jnp.where(low, 0.0, qg).astype(jnp.bfloat16)
            kv_s[b] = kv.astype(jnp.bfloat16)
            kt = (kv.T[:HD] * scale).astype(jnp.bfloat16)
            kt_s[b, :HD] = kt
            kt_s[b, HD:] = kt
            dkv_s[b] = jnp.zeros((BS, 2 * HD), jnp.float32)

    def one_block(b, count, slots):
        qg = qg_s[b]
        listed = [block_ref[b, j] for j in range(slots)]
        top = None
        for j in range(slots):
            sd = lax.dot_general(kv_s[listed[j]], qg, NT, preferred_element_type=jnp.float32)
            s = sd[:, :BS]
            if j > slots - STEP:
                s = jnp.where(j < count, s, -jnp.inf)
            s_s[j] = s
            d_s[j] = sd[:, BS:]
            top = s if top is None else jnp.maximum(top, s)
        top = jnp.max(top, axis=0, keepdims=True)
        norm = weighted = None
        for j in range(slots):
            e = jnp.exp(s_s[j] - top)
            s_s[j] = e
            ed = e * d_s[j]
            norm = e if norm is None else norm + e
            weighted = ed if weighted is None else weighted + ed
        inv = 1.0 / jnp.sum(norm, axis=0, keepdims=True)
        delta = jnp.sum(weighted, axis=0, keepdims=True) * inv
        dqt = None
        for j in range(0, slots, 2):
            ds_pair = []
            updates = []
            for k in (j, j + 1):
                p = s_s[k] * inv
                ds = (p * (d_s[k] - delta)).astype(jnp.bfloat16)
                ds_pair.append(ds)
                updates.append(dot(jnp.concatenate((ds, p.astype(jnp.bfloat16)), axis=1), qg))
            kt = jnp.concatenate((kt_s[listed[j]], kt_s[listed[j + 1]]), axis=1)
            term = dot(kt, jnp.concatenate(ds_pair, axis=0))
            dqt = term if dqt is None else dqt + term
            for k in (0, 1):
                dkv_s[listed[j + k]] += updates[k]
        g_s[pl.ds(pl.multiple_of(b * BS, BS), BS), 2 * HD:] = dqt.T.astype(jnp.bfloat16)

    @pl.loop(0, block_count)
    def _(b):
        count = count_ref[b]
        for slots in range(STEP, KB + 1, STEP):
            @pl.when((count > slots - STEP) & (count <= slots))
            def _():
                one_block(b, count, slots)

    @pl.loop(0, block_count)
    def _(b):
        g_s[pl.ds(pl.multiple_of(b * BS, BS), BS), :2 * HD] = dkv_s[b].astype(jnp.bfloat16)

    @pl.loop(0, parts)
    def _(i):
        halves = []
        for u in range(2):
            start = pl.multiple_of((i * 2 + u) * half, half)
            ids = lax.broadcasted_iota(jnp.int32, (half, nodes), 1)
            hot = jnp.where(ids == col_ref[pl.ds(start, half), :], 1.0, 0.0).astype(jnp.bfloat16)
            got = dot(hot, g_s[...])
            out_ref[i, u * half:(u + 1) * half] = got[:, :2 * HD].astype(jnp.bfloat16)
            halves.append(got[:, 2 * HD:])
        keep = lax.broadcasted_iota(jnp.int32, (half, 2 * HD), 1) < HD
        out_ref[i, 2 * half:] = jnp.where(keep, halves[0], halves[1]).astype(jnp.bfloat16)


def attention(x, order, block_row, count_row, parts):
    nodes = x.shape[0]
    block_count = nodes // BS
    vmem = pl.BlockSpec(memory_space=pltpu.VMEM)
    smem = pl.BlockSpec(memory_space=pltpu.SMEM)
    return pl.pallas_call(
        attend,
        out_shape=jax.ShapeDtypeStruct((parts, nodes // parts * 3 // 2, 2 * HD), jnp.bfloat16),
        in_specs=[smem, smem, vmem, vmem, vmem],
        out_specs=vmem,
        scratch_shapes=[
            pltpu.VMEM((block_count, BS, 2 * HD), jnp.bfloat16),
            pltpu.VMEM((block_count, 2 * HD, BS), jnp.bfloat16),
            pltpu.VMEM((block_count, 2 * BS, 2 * HD), jnp.bfloat16),
            pltpu.VMEM((block_count, BS, 2 * HD), jnp.float32),
            pltpu.VMEM((nodes, 4 * HD), jnp.bfloat16),
            pltpu.VMEM((KB, BS, BS), jnp.float32),
            pltpu.VMEM((KB, BS, BS), jnp.float32),
        ],
        compiler_params=pltpu.CompilerParams(vmem_limit_bytes=48 << 20),
        name="attend",
    )(block_row, count_row, order.reshape(1, nodes), order.reshape(nodes, 1), x)


def project(side_ref, rec_ref, wq_ref, wk_ref, wv_ref, keep_ref, send_ref, aq, ak, av):
    heads, out_rows, _ = rec_ref.shape
    half = out_rows // 3
    for h in range(heads):
        cols = slice(h * HD, (h + 1) * HD)
        aq[:half, cols] = rec_ref[h, 2 * half:, :HD]
        aq[half:, cols] = rec_ref[h, 2 * half:, HD:]
        ak[:, cols] = rec_ref[h, :2 * half, :HD]
        av[:, cols] = rec_ref[h, :2 * half, HD:]
    side = side_ref[0]

    def rows_at(part):
        rows = pl.ds(pl.multiple_of(part * half, half), half)
        total = lax.dot_general(aq[rows], wq_ref[...], NT, preferred_element_type=jnp.float32)
        total += lax.dot_general(ak[rows], wk_ref[...], NT, preferred_element_type=jnp.float32)
        total += lax.dot_general(av[rows], wv_ref[...], NT, preferred_element_type=jnp.float32)
        return total

    send_ref[...] = rows_at(1 - side).astype(jnp.bfloat16)
    keep_ref[...] = rows_at(side)


def projection(side, received, w_query, w_key, w_value, graphs):
    total_heads, out_rows, _ = received.shape
    heads = total_heads // graphs
    half = out_rows // 3
    full, width = w_query.shape
    weight = pl.BlockSpec((full, width), lambda g: (0, 0))
    result = pl.BlockSpec((None, half, full), lambda g: (g, 0, 0))
    return pl.pallas_call(
        project,
        grid=(graphs,),
        out_shape=(
            jax.ShapeDtypeStruct((graphs, half, full), jnp.float32),
            jax.ShapeDtypeStruct((graphs, half, full), jnp.bfloat16),
        ),
        in_specs=[
            pl.BlockSpec(memory_space=pltpu.SMEM),
            pl.BlockSpec((heads, out_rows, 2 * HD), lambda g: (g, 0, 0)),
            weight, weight, weight,
        ],
        out_specs=(result, result),
        scratch_shapes=[pltpu.VMEM((2 * half, width), jnp.bfloat16)] * 3,
        compiler_params=pltpu.CompilerParams(vmem_limit_bytes=48 << 20),
        name="project",
    )(side, received, w_query, w_key, w_value)


def on_device(
    query, keys_in, values_in, grad_out, w_out, w_query, w_key, w_value, perm, blocks, counts
):
    local_rows, half_width = query.shape
    graphs, nodes = perm.shape
    half_heads = half_width // HD
    part_rows = local_rows // graphs
    parts = nodes // part_rows
    attn_grad = lax.dot_general(
        lax.all_gather(grad_out, "tensor", axis=1, tiled=True),
        w_out,
        NT,
        preferred_element_type=jnp.float32,
    ).astype(jnp.bfloat16)
    packed = jnp.concatenate(
        [
            member.reshape(part_rows, graphs * half_heads, HD).transpose(1, 0, 2)
            for member in (query, attn_grad, keys_in, values_in)
        ],
        axis=2,
    )
    arrived = lax.all_to_all(packed, "head", split_axis=0, concat_axis=0, tiled=True)
    graph = lax.axis_index("head") // half_heads
    order = lax.dynamic_index_in_dim(perm, graph, 0, keepdims=False)
    block_row = lax.dynamic_index_in_dim(blocks, graph, 0, keepdims=False)
    count_row = lax.dynamic_index_in_dim(counts, graph, 0, keepdims=False)
    by_part = attention(arrived.reshape(nodes, 4 * HD), order, block_row, count_row, parts)
    returned = lax.all_to_all(by_part, "head", split_axis=0, concat_axis=0, tiled=True)
    side = lax.axis_index("tensor").astype(jnp.int32).reshape(1)
    keep, send = projection(side, returned, w_query, w_key, w_value, graphs)
    got = lax.ppermute(send, "tensor", [(0, 1), (1, 0)])
    total = (keep + got.astype(jnp.float32)).astype(jnp.bfloat16)
    return total.transpose(1, 0, 2).reshape(local_rows // 2, -1)


def solution(mesh):
    return jax.shard_map(
        on_device,
        mesh=mesh,
        in_specs=(
            P(("groups", "head"), "tensor"),
            P(("groups", "head"), "tensor"),
            P(("groups", "head"), "tensor"),
            P(("groups", "head"), "tensor"),
            P("tensor", None),
            P(None, "tensor"),
            P(None, "tensor"),
            P(None, "tensor"),
            P("groups", None),
            P("groups", None, None),
            P("groups", None),
        ),
        out_specs=P(("groups", "head", "tensor"), None),
        check_vma=False,
    )
```

```python
import jax
import jax.numpy as jnp
from jax import lax
from jax.experimental import pallas as pl
from jax.experimental.pallas import tpu as pltpu
from jax.sharding import PartitionSpec as P

HD = 64
BS = 128
KB = 12
NT = (((1,), (1,)), ((), ()))
STEP = 4
TILE = 512
MESH = pl.DeviceIdType.MESH


def dot(a, b):
    return jnp.dot(a, b, preferred_element_type=jnp.float32)


def spread(row_ref, q_ref, k_ref, v_ref, go_ref, w_ref, qg_out, kv_out,
           grad_s, attn_s, kv_pack, qg_pack, kv_in, qg_in, acc_s, pair_sem, send_sem, recv_sem):
    n, part_rows, _ = kv_in.shape
    heads = q_ref.shape[1] // HD
    graphs = n // heads
    nodes = n * part_rows
    me = lax.axis_index("head")
    side = lax.axis_index("tensor")
    width = go_ref.shape[1]
    barrier = pltpu.get_barrier_semaphore()
    pl.semaphore_signal(barrier, inc=1, device_id={"tensor": 1 - side}, device_id_type=MESH)

    @pl.loop(1, n)
    def _(k):
        pl.semaphore_signal(barrier, inc=1, device_id={"head": lax.rem(me + k, n)}, device_id_type=MESH)

    @pl.loop(0, graphs)
    def _(g):
        rows = pl.ds(pl.multiple_of(g * part_rows, part_rows), part_rows)
        for h in range(heads):
            cols = slice(h * HD, (h + 1) * HD)
            kv_pack[g * heads + h, :, :HD] = k_ref[rows, cols]
            kv_pack[g * heads + h, :, HD:] = v_ref[rows, cols]
            qg_pack[g * heads + h, :, :HD] = q_ref[rows, cols]

    pl.semaphore_wait(barrier, n)
    pair = pltpu.make_async_remote_copy(
        src_ref=go_ref, dst_ref=grad_s, send_sem=pair_sem.at[0], recv_sem=pair_sem.at[1],
        device_id={"tensor": 1 - side}, device_id_type=MESH,
    )
    pair.start()

    def copy_to(which, pack, land, peer, slot):
        return pltpu.make_async_remote_copy(
            src_ref=pack.at[peer], dst_ref=land.at[slot],
            send_sem=send_sem.at[which, peer], recv_sem=recv_sem.at[which, slot],
            device_id={"head": peer}, device_id_type=MESH,
        )

    def send_all(which, pack, land):
        @pl.loop(1, n)
        def _(k):
            copy_to(which, pack, land, lax.rem(me + k, n), me).start()

    send_all(0, kv_pack, kv_in)
    near = pl.ds(pl.multiple_of(side * width, width), width)
    far = pl.ds(pl.multiple_of((1 - side) * width, width), width)
    attn_s[...] = lax.dot_general(go_ref[...], w_ref[:, near], NT, preferred_element_type=jnp.float32)
    pair.wait()
    attn_s[...] += lax.dot_general(grad_s[...], w_ref[:, far], NT, preferred_element_type=jnp.float32)

    @pl.loop(0, graphs)
    def _(g):
        rows = pl.ds(pl.multiple_of(g * part_rows, part_rows), part_rows)
        for h in range(heads):
            cols = slice(h * HD, (h + 1) * HD)
            qg_pack[g * heads + h, :, HD:] = attn_s[rows, cols].astype(jnp.bfloat16)

    send_all(1, qg_pack, qg_in)

    def gather(which, pack, land, out):
        def add(chunk, source, first):
            @pl.loop(0, nodes // TILE)
            def _(i):
                rows = pl.ds(pl.multiple_of(i * TILE, TILE), TILE)
                ids = lax.broadcasted_iota(jnp.int32, (TILE, part_rows), 0) + i * TILE
                hot = jnp.where(ids == row_ref[source], 1.0, 0.0).astype(jnp.bfloat16)
                if first:
                    acc_s[rows] = dot(hot, chunk)
                else:
                    acc_s[rows] += dot(hot, chunk)

        add(pack[me], me, True)

        @pl.loop(1, n)
        def _(k):
            source = lax.rem(me + n - k, n)
            copy_to(which, pack, land, source, source).wait_recv()
            add(land[source], source, False)

        out[...] = acc_s[...].astype(jnp.bfloat16)

    gather(0, kv_pack, kv_in, kv_out)
    gather(1, qg_pack, qg_in, qg_out)

    @pl.loop(1, n)
    def _(k):
        peer = lax.rem(me + k, n)
        copy_to(0, kv_pack, kv_in, peer, me).wait_send()
        copy_to(1, qg_pack, qg_in, peer, me).wait_send()


def spreading(order, query, keys_in, values_in, grad_out, w_out, n):
    nodes = order.shape[0]
    part_rows = nodes // n
    vmem = pl.BlockSpec(memory_space=pltpu.VMEM)
    chunks = pltpu.VMEM((n, part_rows, 2 * HD), jnp.bfloat16)
    half = jax.ShapeDtypeStruct((nodes, 2 * HD), jnp.bfloat16)
    return pl.pallas_call(
        spread,
        out_shape=(half, half),
        in_specs=[vmem] * 6,
        out_specs=(vmem, vmem),
        scratch_shapes=[
            pltpu.VMEM(grad_out.shape, jnp.bfloat16),
            pltpu.VMEM(query.shape, jnp.float32),
            chunks, chunks, chunks, chunks,
            pltpu.VMEM((nodes, 2 * HD), jnp.float32),
            pltpu.SemaphoreType.DMA((2,)),
            pltpu.SemaphoreType.DMA((2, n)),
            pltpu.SemaphoreType.DMA((2, n)),
        ],
        compiler_params=pltpu.CompilerParams(
            vmem_limit_bytes=48 << 20, collective_id=0, has_side_effects=True
        ),
        name="spread",
    )(order.reshape(n, 1, part_rows), query, keys_in, values_in, grad_out, w_out)


def attend(block_ref, count_ref, qg_ref, kv_ref, out_ref, kt_s, qg_s, dkv_s, s_s, d_s):
    block_count = kv_ref.shape[0]
    scale = HD ** (-0.5)
    low = lax.broadcasted_iota(jnp.int32, (BS, 2 * HD), 1) < HD

    @pl.loop(0, block_count)
    def _(b):
        qg = qg_ref[b].astype(jnp.float32)
        qg_s[b, :BS] = jnp.where(low, qg * scale, 0.0).astype(jnp.bfloat16)
        qg_s[b, BS:] = jnp.where(low, 0.0, qg).astype(jnp.bfloat16)
        kt = (kv_ref[b].astype(jnp.float32).T[:HD] * scale).astype(jnp.bfloat16)
        kt_s[b, :HD] = kt
        kt_s[b, HD:] = kt
        dkv_s[b] = jnp.zeros((BS, 2 * HD), jnp.float32)

    def one_block(b, count, slots):
        qg = qg_s[b]
        listed = [block_ref[b, j] for j in range(slots)]
        top = None
        for j in range(slots):
            sd = lax.dot_general(kv_ref[listed[j]], qg, NT, preferred_element_type=jnp.float32)
            s = sd[:, :BS]
            if j > slots - STEP:
                s = jnp.where(j < count, s, -jnp.inf)
            s_s[j] = s
            d_s[j] = sd[:, BS:]
            top = s if top is None else jnp.maximum(top, s)
        top = jnp.max(top, axis=0, keepdims=True)
        norm = weighted = None
        for j in range(slots):
            e = jnp.exp(s_s[j] - top)
            s_s[j] = e
            ed = e * d_s[j]
            norm = e if norm is None else norm + e
            weighted = ed if weighted is None else weighted + ed
        inv = 1.0 / jnp.sum(norm, axis=0, keepdims=True)
        delta = jnp.sum(weighted, axis=0, keepdims=True) * inv
        dqt = None
        for j in range(0, slots, 2):
            ds_pair = []
            updates = []
            for k in (j, j + 1):
                p = s_s[k] * inv
                ds = (p * (d_s[k] - delta)).astype(jnp.bfloat16)
                ds_pair.append(ds)
                updates.append(dot(jnp.concatenate((ds, p.astype(jnp.bfloat16)), axis=1), qg))
            kt = jnp.concatenate((kt_s[listed[j]], kt_s[listed[j + 1]]), axis=1)
            term = dot(kt, jnp.concatenate(ds_pair, axis=0))
            dqt = term if dqt is None else dqt + term
            for k in (0, 1):
                dkv_s[listed[j + k]] += updates[k]
        out_ref[pl.ds(pl.multiple_of(b * BS, BS), BS), 2 * HD:] = dqt.T.astype(jnp.bfloat16)

    @pl.loop(0, block_count)
    def _(b):
        count = count_ref[b]
        for slots in range(STEP, KB + 1, STEP):
            @pl.when((count > slots - STEP) & (count <= slots))
            def _():
                one_block(b, count, slots)

    @pl.loop(0, block_count)
    def _(b):
        out_ref[pl.ds(pl.multiple_of(b * BS, BS), BS), :2 * HD] = dkv_s[b].astype(jnp.bfloat16)


def attention(qg, kv, block_row, count_row):
    nodes = qg.shape[0]
    block_count = nodes // BS
    vmem = pl.BlockSpec(memory_space=pltpu.VMEM)
    smem = pl.BlockSpec(memory_space=pltpu.SMEM)
    return pl.pallas_call(
        attend,
        out_shape=jax.ShapeDtypeStruct((nodes, 4 * HD), jnp.bfloat16),
        in_specs=[smem, smem, vmem, vmem],
        out_specs=vmem,
        scratch_shapes=[
            pltpu.VMEM((block_count, 2 * HD, BS), jnp.bfloat16),
            pltpu.VMEM((block_count, 2 * BS, 2 * HD), jnp.bfloat16),
            pltpu.VMEM((block_count, BS, 2 * HD), jnp.float32),
            pltpu.VMEM((KB, BS, BS), jnp.float32),
            pltpu.VMEM((KB, BS, BS), jnp.float32),
        ],
        compiler_params=pltpu.CompilerParams(vmem_limit_bytes=48 << 20),
        name="attend",
    )(block_row, count_row, qg.reshape(block_count, BS, 2 * HD), kv.reshape(block_count, BS, 2 * HD))


def collect(col_ref, g_ref, wq_ref, wk_ref, wv_ref, out_ref,
            pack, land, aq, ak, av, keep_s, give_s, got_s, pair_sem, send_sem, recv_sem):
    n, out_rows, _ = land.shape
    half = out_rows // 3
    graphs = out_ref.shape[0]
    heads = n // graphs
    nodes = g_ref.shape[0]
    me = lax.axis_index("head")
    side = lax.axis_index("tensor")
    barrier = pltpu.get_barrier_semaphore()
    pl.semaphore_signal(barrier, inc=1, device_id={"tensor": 1 - side}, device_id_type=MESH)

    @pl.loop(1, n)
    def _(k):
        pl.semaphore_signal(barrier, inc=1, device_id={"head": lax.rem(me + k, n)}, device_id_type=MESH)

    def make(peer, into):
        halves = []
        for u in range(2):
            start = pl.multiple_of((peer * 2 + u) * half, half)
            ids = lax.broadcasted_iota(jnp.int32, (half, nodes), 1)
            hot = jnp.where(ids == col_ref[pl.ds(start, half), :], 1.0, 0.0).astype(jnp.bfloat16)
            got = dot(hot, g_ref[...])
            into[u * half:(u + 1) * half] = got[:, :2 * HD].astype(jnp.bfloat16)
            halves.append(got[:, 2 * HD:])
        low = lax.broadcasted_iota(jnp.int32, (half, 2 * HD), 1) < HD
        into[2 * half:] = jnp.where(low, halves[0], halves[1]).astype(jnp.bfloat16)

    def copy_to(peer, slot):
        return pltpu.make_async_remote_copy(
            src_ref=pack.at[peer], dst_ref=land.at[slot],
            send_sem=send_sem.at[peer], recv_sem=recv_sem.at[slot],
            device_id={"head": peer}, device_id_type=MESH,
        )

    pl.semaphore_wait(barrier, n)

    @pl.loop(1, n)
    def _(k):
        peer = lax.rem(me + k, n)
        make(peer, pack.at[peer])
        copy_to(peer, me).start()

    make(me, land.at[me])

    @pl.loop(1, n)
    def _(k):
        source = lax.rem(me + n - k, n)
        copy_to(source, source).wait_recv()

    @pl.loop(0, graphs)
    def _(g):
        for h in range(heads):
            cols = slice(h * HD, (h + 1) * HD)
            slot = g * heads + h
            aq[:half, cols] = land[slot, 2 * half:, :HD]
            aq[half:, cols] = land[slot, 2 * half:, HD:]
            ak[:, cols] = land[slot, :2 * half, :HD]
            av[:, cols] = land[slot, :2 * half, HD:]

        def rows_at(part):
            rows = pl.ds(pl.multiple_of(part * half, half), half)
            total = lax.dot_general(aq[rows], wq_ref[...], NT, preferred_element_type=jnp.float32)
            total += lax.dot_general(ak[rows], wk_ref[...], NT, preferred_element_type=jnp.float32)
            total += lax.dot_general(av[rows], wv_ref[...], NT, preferred_element_type=jnp.float32)
            return total

        give_s[g] = rows_at(1 - side).astype(jnp.bfloat16)
        keep_s[g] = rows_at(side)

    pair = pltpu.make_async_remote_copy(
        src_ref=give_s, dst_ref=got_s, send_sem=pair_sem.at[0], recv_sem=pair_sem.at[1],
        device_id={"tensor": 1 - side}, device_id_type=MESH,
    )
    pair.start()
    pair.wait()
    out_ref[...] = (keep_s[...] + got_s[...].astype(jnp.float32)).astype(jnp.bfloat16)

    @pl.loop(1, n)
    def _(k):
        copy_to(lax.rem(me + k, n), me).wait_send()


def collecting(order, grads, w_query, w_key, w_value, graphs, n):
    nodes = order.shape[0]
    part_rows = nodes // n
    full, width = w_query.shape
    vmem = pl.BlockSpec(memory_space=pltpu.VMEM)
    chunks = pltpu.VMEM((n, part_rows * 3 // 2, 2 * HD), jnp.bfloat16)
    result = (graphs, part_rows // 2, full)
    return pl.pallas_call(
        collect,
        out_shape=jax.ShapeDtypeStruct(result, jnp.bfloat16),
        in_specs=[vmem] * 5,
        out_specs=vmem,
        scratch_shapes=[
            chunks, chunks,
            pltpu.VMEM((part_rows, width), jnp.bfloat16),
            pltpu.VMEM((part_rows, width), jnp.bfloat16),
            pltpu.VMEM((part_rows, width), jnp.bfloat16),
            pltpu.VMEM(result, jnp.float32),
            pltpu.VMEM(result, jnp.bfloat16),
            pltpu.VMEM(result, jnp.bfloat16),
            pltpu.SemaphoreType.DMA((2,)),
            pltpu.SemaphoreType.DMA((n,)),
            pltpu.SemaphoreType.DMA((n,)),
        ],
        compiler_params=pltpu.CompilerParams(
            vmem_limit_bytes=48 << 20, collective_id=1, has_side_effects=True
        ),
        name="collect",
    )(order.reshape(nodes, 1), grads, w_query, w_key, w_value)


def on_device(
    query, keys_in, values_in, grad_out, w_out, w_query, w_key, w_value, perm, blocks, counts
):
    local_rows, half_width = query.shape
    graphs, nodes = perm.shape
    half_heads = half_width // HD
    part_rows = local_rows // graphs
    n = nodes // part_rows
    graph = lax.axis_index("head") // half_heads
    order = lax.dynamic_index_in_dim(perm, graph, 0, keepdims=False)
    block_row = lax.dynamic_index_in_dim(blocks, graph, 0, keepdims=False)
    count_row = lax.dynamic_index_in_dim(counts, graph, 0, keepdims=False)
    by_graph = [
        member.reshape(part_rows, graphs, half_width).transpose(1, 0, 2).reshape(local_rows, half_width)
        for member in (query, keys_in, values_in, grad_out)
    ]
    qg, kv = spreading(order, *by_graph, w_out, n)
    grads = attention(qg, kv, block_row, count_row)
    total = collecting(order, grads, w_query, w_key, w_value, graphs, n)
    return total.transpose(1, 0, 2).reshape(local_rows // 2, -1)


def solution(mesh):
    return jax.shard_map(
        on_device,
        mesh=mesh,
        in_specs=(
            P(("groups", "head"), "tensor"),
            P(("groups", "head"), "tensor"),
            P(("groups", "head"), "tensor"),
            P(("groups", "head"), "tensor"),
            P("tensor", None),
            P(None, "tensor"),
            P(None, "tensor"),
            P(None, "tensor"),
            P("groups", None),
            P("groups", None, None),
            P("groups", None),
        ),
        out_specs=P(("groups", "head", "tensor"), None),
        check_vma=False,
    )
```

```python
import jax
import jax.numpy as jnp
from jax import lax
from jax.experimental import pallas as pl
from jax.experimental.pallas import tpu as pltpu
from jax.sharding import PartitionSpec as P

HD = 64
BS = 128
KB = 12
NT = (((1,), (1,)), ((), ()))
STEP = 2
VMEM_BYTES = 67043328
TILE = 512
MESH = pl.DeviceIdType.MESH


def dot(a, b):
    return jnp.dot(a, b, preferred_element_type=jnp.float32)


def hop(i, n):
    return n // 2 + (1 - 2 * lax.rem(i, 2)) * ((i + 1) // 2)


def spread(row_ref, q_hbm, k_hbm, v_hbm, go_hbm, w_hbm, qg_out, kv_out,
           q_ref, k_ref, v_ref, go_ref, w_ref, load_sem, grad_s, attn_s, kv_pack, qg_pack, kv_in, qg_in, acc_s, pair_sem, send_sem, recv_sem):
    n, part_rows, _ = kv_in.shape
    heads = q_ref.shape[1] // HD
    graphs = n // heads
    nodes = n * part_rows
    me = lax.axis_index("head")
    side = lax.axis_index("tensor")
    width = go_ref.shape[1]
    loads = [
        pltpu.make_async_copy(src, dst, load_sem.at[at])
        for at, (src, dst) in enumerate(
            ((k_hbm, k_ref), (v_hbm, v_ref), (go_hbm, go_ref), (q_hbm, q_ref), (w_hbm, w_ref))
        )
    ]
    for load in loads:
        load.start()
    barrier = pltpu.get_barrier_semaphore()
    pl.semaphore_signal(barrier, inc=1, device_id={"tensor": 1 - side}, device_id_type=MESH)

    @pl.loop(1, n)
    def _(k):
        pl.semaphore_signal(barrier, inc=1, device_id={"head": lax.rem(me + k, n)}, device_id_type=MESH)

    loads[0].wait()
    loads[1].wait()

    @pl.loop(0, graphs)
    def _(g):
        rows = pl.ds(pl.multiple_of(g * part_rows, part_rows), part_rows)
        for h in range(heads):
            cols = slice(h * HD, (h + 1) * HD)
            kv_pack[g * heads + h, :, :HD] = k_ref[rows, cols]
            kv_pack[g * heads + h, :, HD:] = v_ref[rows, cols]

    loads[2].wait()
    pl.semaphore_wait(barrier, n)
    pair = pltpu.make_async_remote_copy(
        src_ref=go_ref, dst_ref=grad_s, send_sem=pair_sem.at[0], recv_sem=pair_sem.at[1],
        device_id={"tensor": 1 - side}, device_id_type=MESH,
    )
    pair.start()

    def copy_to(which, pack, land, peer, slot):
        return pltpu.make_async_remote_copy(
            src_ref=pack.at[peer], dst_ref=land.at[slot],
            send_sem=send_sem.at[which, peer], recv_sem=recv_sem.at[which, slot],
            device_id={"head": peer}, device_id_type=MESH,
        )

    def send_all(which, pack, land):
        @pl.loop(0, n - 1)
        def _(i):
            copy_to(which, pack, land, lax.rem(me + hop(i, n), n), me).start()

    send_all(0, kv_pack, kv_in)
    loads[3].wait()
    loads[4].wait()
    near = pl.ds(pl.multiple_of(side * width, width), width)
    far = pl.ds(pl.multiple_of((1 - side) * width, width), width)
    attn_s[...] = lax.dot_general(go_ref[...], w_ref[:, near], NT, preferred_element_type=jnp.float32)
    pair.wait()
    attn_s[...] += lax.dot_general(grad_s[...], w_ref[:, far], NT, preferred_element_type=jnp.float32)

    @pl.loop(0, graphs)
    def _(g):
        rows = pl.ds(pl.multiple_of(g * part_rows, part_rows), part_rows)
        for h in range(heads):
            cols = slice(h * HD, (h + 1) * HD)
            qg_pack[g * heads + h, :, :HD] = q_ref[rows, cols]
            qg_pack[g * heads + h, :, HD:] = attn_s[rows, cols].astype(jnp.bfloat16)

    send_all(1, qg_pack, qg_in)

    def gather(which, pack, land, out):
        def add(chunk, source, first):
            @pl.loop(0, nodes // TILE)
            def _(i):
                rows = pl.ds(pl.multiple_of(i * TILE, TILE), TILE)
                ids = lax.broadcasted_iota(jnp.int32, (TILE, part_rows), 0) + i * TILE
                hot = jnp.where(ids == row_ref[source], 1.0, 0.0).astype(jnp.bfloat16)
                if first:
                    acc_s[rows] = dot(hot, chunk)
                else:
                    acc_s[rows] += dot(hot, chunk)

        add(pack[me], me, True)

        @pl.loop(0, n - 1)
        def _(i):
            source = lax.rem(me + n - hop(i, n), n)
            copy_to(which, pack, land, source, source).wait_recv()
            add(land[source], source, False)

        out[...] = acc_s[...].astype(jnp.bfloat16)

    gather(0, kv_pack, kv_in, kv_out)
    gather(1, qg_pack, qg_in, qg_out)

    @pl.loop(1, n)
    def _(k):
        peer = lax.rem(me + k, n)
        copy_to(0, kv_pack, kv_in, peer, me).wait_send()
        copy_to(1, qg_pack, qg_in, peer, me).wait_send()


def spreading(order, query, keys_in, values_in, grad_out, w_out, n):
    nodes = order.shape[0]
    part_rows = nodes // n
    vmem = pl.BlockSpec(memory_space=pltpu.VMEM)
    chunks = pltpu.VMEM((n, part_rows, 2 * HD), jnp.bfloat16)
    half = jax.ShapeDtypeStruct((nodes, 2 * HD), jnp.bfloat16)
    return pl.pallas_call(
        spread,
        out_shape=(half, half),
        in_specs=[vmem] + [pl.BlockSpec(memory_space=pltpu.HBM)] * 5,
        out_specs=(vmem, vmem),
        scratch_shapes=[
            pltpu.VMEM(query.shape, jnp.bfloat16),
            pltpu.VMEM(query.shape, jnp.bfloat16),
            pltpu.VMEM(query.shape, jnp.bfloat16),
            pltpu.VMEM(grad_out.shape, jnp.bfloat16),
            pltpu.VMEM(w_out.shape, jnp.bfloat16),
            pltpu.SemaphoreType.DMA((5,)),
            pltpu.VMEM(grad_out.shape, jnp.bfloat16),
            pltpu.VMEM(query.shape, jnp.float32),
            chunks, chunks, chunks, chunks,
            pltpu.VMEM((nodes, 2 * HD), jnp.float32),
            pltpu.SemaphoreType.DMA((2,)),
            pltpu.SemaphoreType.DMA((2, n)),
            pltpu.SemaphoreType.DMA((2, n)),
        ],
        compiler_params=pltpu.CompilerParams(
            vmem_limit_bytes=VMEM_BYTES, collective_id=0, has_side_effects=True
        ),
        name="spread",
    )(order.reshape(n, 1, part_rows), query, keys_in, values_in, grad_out, w_out)


def attend(block_ref, count_ref, qg_ref, kv_ref, out_ref, kt_s, qg_s, dkv_s, s_s, d_s):
    block_count = kv_ref.shape[0]
    scale = HD ** (-0.5)
    low = lax.broadcasted_iota(jnp.int32, (BS, 2 * HD), 1) < HD

    @pl.loop(0, block_count)
    def _(b):
        qg = qg_ref[b].astype(jnp.float32)
        qg_s[b, :BS] = jnp.where(low, qg * scale, 0.0).astype(jnp.bfloat16)
        qg_s[b, BS:] = jnp.where(low, 0.0, qg).astype(jnp.bfloat16)
        kt = (kv_ref[b].astype(jnp.float32).T[:HD] * scale).astype(jnp.bfloat16)
        kt_s[b, :HD] = kt
        kt_s[b, HD:] = kt
        dkv_s[b] = jnp.zeros((BS, 2 * HD), jnp.float32)

    def one_block(b, count, slots):
        qg = qg_s[b]
        listed = [block_ref[b, j] for j in range(slots)]
        top = None
        for j in range(slots):
            sd = lax.dot_general(kv_ref[listed[j]], qg, NT, preferred_element_type=jnp.float32)
            s = sd[:, :BS]
            if j > slots - STEP:
                s = jnp.where(j < count, s, -jnp.inf)
            s_s[j] = s
            d_s[j] = sd[:, BS:]
            top = s if top is None else jnp.maximum(top, s)
        top = jnp.max(top, axis=0, keepdims=True)
        norm = weighted = None
        for j in range(slots):
            e = jnp.exp(s_s[j] - top)
            s_s[j] = e
            ed = e * d_s[j]
            norm = e if norm is None else norm + e
            weighted = ed if weighted is None else weighted + ed
        inv = 1.0 / jnp.sum(norm, axis=0, keepdims=True)
        delta = jnp.sum(weighted, axis=0, keepdims=True) * inv
        dqt = None
        for j in range(0, slots, 2):
            ds_pair = []
            updates = []
            for k in (j, j + 1):
                p = s_s[k] * inv
                ds = (p * (d_s[k] - delta)).astype(jnp.bfloat16)
                ds_pair.append(ds)
                updates.append(dot(jnp.concatenate((ds, p.astype(jnp.bfloat16)), axis=1), qg))
            kt = jnp.concatenate((kt_s[listed[j]], kt_s[listed[j + 1]]), axis=1)
            term = dot(kt, jnp.concatenate(ds_pair, axis=0))
            dqt = term if dqt is None else dqt + term
            for k in (0, 1):
                dkv_s[listed[j + k]] += updates[k]
        out_ref[pl.ds(pl.multiple_of(b * BS, BS), BS), 2 * HD:] = dqt.T.astype(jnp.bfloat16)

    @pl.loop(0, block_count)
    def _(b):
        count = count_ref[b]
        for slots in range(STEP, KB + 1, STEP):
            @pl.when((count > slots - STEP) & (count <= slots))
            def _():
                one_block(b, count, slots)

    @pl.loop(0, block_count)
    def _(b):
        out_ref[pl.ds(pl.multiple_of(b * BS, BS), BS), :2 * HD] = dkv_s[b].astype(jnp.bfloat16)


def attention(qg, kv, block_row, count_row):
    nodes = qg.shape[0]
    block_count = nodes // BS
    vmem = pl.BlockSpec(memory_space=pltpu.VMEM)
    smem = pl.BlockSpec(memory_space=pltpu.SMEM)
    return pl.pallas_call(
        attend,
        out_shape=jax.ShapeDtypeStruct((nodes, 4 * HD), jnp.bfloat16),
        in_specs=[smem, smem, vmem, vmem],
        out_specs=vmem,
        scratch_shapes=[
            pltpu.VMEM((block_count, 2 * HD, BS), jnp.bfloat16),
            pltpu.VMEM((block_count, 2 * BS, 2 * HD), jnp.bfloat16),
            pltpu.VMEM((block_count, BS, 2 * HD), jnp.float32),
            pltpu.VMEM((KB, BS, BS), jnp.float32),
            pltpu.VMEM((KB, BS, BS), jnp.float32),
        ],
        compiler_params=pltpu.CompilerParams(vmem_limit_bytes=VMEM_BYTES),
        name="attend",
    )(block_row, count_row, qg.reshape(block_count, BS, 2 * HD), kv.reshape(block_count, BS, 2 * HD))


def collect(col_ref, g_ref, wq_hbm, wk_hbm, wv_hbm, out_ref,
            wq_ref, wk_ref, wv_ref, load_sem, pack, land, aq, ak, av, keep_s, give_s, got_s, pair_sem, send_sem, recv_sem):
    n, out_rows, _ = land.shape
    half = out_rows // 3
    graphs = out_ref.shape[0]
    heads = n // graphs
    nodes = g_ref.shape[0]
    me = lax.axis_index("head")
    side = lax.axis_index("tensor")
    loads = [
        pltpu.make_async_copy(src, dst, load_sem.at[at])
        for at, (src, dst) in enumerate(((wq_hbm, wq_ref), (wk_hbm, wk_ref), (wv_hbm, wv_ref)))
    ]
    for load in loads:
        load.start()
    barrier = pltpu.get_barrier_semaphore()
    pl.semaphore_signal(barrier, inc=1, device_id={"tensor": 1 - side}, device_id_type=MESH)

    @pl.loop(1, n)
    def _(k):
        pl.semaphore_signal(barrier, inc=1, device_id={"head": lax.rem(me + k, n)}, device_id_type=MESH)

    def make(peer, into):
        halves = []
        for u in range(2):
            start = pl.multiple_of((peer * 2 + u) * half, half)
            ids = lax.broadcasted_iota(jnp.int32, (half, nodes), 1)
            hot = jnp.where(ids == col_ref[pl.ds(start, half), :], 1.0, 0.0).astype(jnp.bfloat16)
            got = dot(hot, g_ref[...])
            into[u * half:(u + 1) * half] = got[:, :2 * HD].astype(jnp.bfloat16)
            halves.append(got[:, 2 * HD:])
        low = lax.broadcasted_iota(jnp.int32, (half, 2 * HD), 1) < HD
        into[2 * half:] = jnp.where(low, halves[0], halves[1]).astype(jnp.bfloat16)

    def copy_to(peer, slot):
        return pltpu.make_async_remote_copy(
            src_ref=pack.at[peer], dst_ref=land.at[slot],
            send_sem=send_sem.at[peer], recv_sem=recv_sem.at[slot],
            device_id={"head": peer}, device_id_type=MESH,
        )

    opposite = lax.rem(me + n // 2, n)
    make(opposite, pack.at[opposite])
    pl.semaphore_wait(barrier, n)
    copy_to(opposite, me).start()

    @pl.loop(1, n - 1)
    def _(i):
        peer = lax.rem(me + hop(i, n), n)
        make(peer, pack.at[peer])
        copy_to(peer, me).start()

    make(me, land.at[me])

    @pl.loop(1, n)
    def _(k):
        source = lax.rem(me + n - k, n)
        copy_to(source, source).wait_recv()

    for load in loads:
        load.wait()

    def rows_at(g, part):
        rows = pl.ds(pl.multiple_of(part * half, half), half)
        total = lax.dot_general(aq[g, rows], wq_ref[...], NT, preferred_element_type=jnp.float32)
        total += lax.dot_general(ak[g, rows], wk_ref[...], NT, preferred_element_type=jnp.float32)
        total += lax.dot_general(av[g, rows], wv_ref[...], NT, preferred_element_type=jnp.float32)
        return total

    @pl.loop(0, graphs)
    def _(g):
        for h in range(heads):
            cols = slice(h * HD, (h + 1) * HD)
            slot = g * heads + h
            aq[g, :half, cols] = land[slot, 2 * half:, :HD]
            aq[g, half:, cols] = land[slot, 2 * half:, HD:]
            ak[g, :, cols] = land[slot, :2 * half, :HD]
            av[g, :, cols] = land[slot, :2 * half, HD:]

        give_s[g] = rows_at(g, 1 - side).astype(jnp.bfloat16)

    pair = pltpu.make_async_remote_copy(
        src_ref=give_s, dst_ref=got_s, send_sem=pair_sem.at[0], recv_sem=pair_sem.at[1],
        device_id={"tensor": 1 - side}, device_id_type=MESH,
    )
    pair.start()

    @pl.loop(0, graphs)
    def _(g):
        keep_s[g] = rows_at(g, side)

    pair.wait()
    out_ref[...] = (keep_s[...] + got_s[...].astype(jnp.float32)).astype(jnp.bfloat16)

    @pl.loop(1, n)
    def _(k):
        copy_to(lax.rem(me + k, n), me).wait_send()


def collecting(order, grads, w_query, w_key, w_value, graphs, n):
    nodes = order.shape[0]
    part_rows = nodes // n
    full, width = w_query.shape
    vmem = pl.BlockSpec(memory_space=pltpu.VMEM)
    chunks = pltpu.VMEM((n, part_rows * 3 // 2, 2 * HD), jnp.bfloat16)
    result = (graphs, part_rows // 2, full)
    return pl.pallas_call(
        collect,
        out_shape=jax.ShapeDtypeStruct(result, jnp.bfloat16),
        in_specs=[vmem] * 2 + [pl.BlockSpec(memory_space=pltpu.HBM)] * 3,
        out_specs=vmem,
        scratch_shapes=[
            pltpu.VMEM(w_query.shape, jnp.bfloat16),
            pltpu.VMEM(w_query.shape, jnp.bfloat16),
            pltpu.VMEM(w_query.shape, jnp.bfloat16),
            pltpu.SemaphoreType.DMA((3,)),
            chunks, chunks,
            pltpu.VMEM((graphs, part_rows, width), jnp.bfloat16),
            pltpu.VMEM((graphs, part_rows, width), jnp.bfloat16),
            pltpu.VMEM((graphs, part_rows, width), jnp.bfloat16),
            pltpu.VMEM(result, jnp.float32),
            pltpu.VMEM(result, jnp.bfloat16),
            pltpu.VMEM(result, jnp.bfloat16),
            pltpu.SemaphoreType.DMA((2,)),
            pltpu.SemaphoreType.DMA((n,)),
            pltpu.SemaphoreType.DMA((n,)),
        ],
        compiler_params=pltpu.CompilerParams(
            vmem_limit_bytes=VMEM_BYTES, collective_id=1, has_side_effects=True
        ),
        name="collect",
    )(order.reshape(nodes, 1), grads, w_query, w_key, w_value)


def on_device(
    query, keys_in, values_in, grad_out, w_out, w_query, w_key, w_value, perm, blocks, counts
):
    local_rows, half_width = query.shape
    graphs, nodes = perm.shape
    half_heads = half_width // HD
    part_rows = local_rows // graphs
    n = nodes // part_rows
    graph = lax.axis_index("head") // half_heads
    order = lax.dynamic_index_in_dim(perm, graph, 0, keepdims=False)
    block_row = lax.dynamic_index_in_dim(blocks, graph, 0, keepdims=False)
    count_row = lax.dynamic_index_in_dim(counts, graph, 0, keepdims=False)
    by_graph = [
        member.reshape(part_rows, graphs, half_width).transpose(1, 0, 2).reshape(local_rows, half_width)
        for member in (query, keys_in, values_in, grad_out)
    ]
    qg, kv = spreading(order, *by_graph, w_out, n)
    grads = attention(qg, kv, block_row, count_row)
    total = collecting(order, grads, w_query, w_key, w_value, graphs, n)
    return total.transpose(1, 0, 2).reshape(local_rows // 2, -1)


def solution(mesh):
    return jax.shard_map(
        on_device,
        mesh=mesh,
        in_specs=(
            P(("groups", "head"), "tensor"),
            P(("groups", "head"), "tensor"),
            P(("groups", "head"), "tensor"),
            P(("groups", "head"), "tensor"),
            P("tensor", None),
            P(None, "tensor"),
            P(None, "tensor"),
            P(None, "tensor"),
            P("groups", None),
            P("groups", None, None),
            P("groups", None),
        ),
        out_specs=P(("groups", "head", "tensor"), None),
        check_vma=False,
    )
```
